128 devices in a mesh: grid: 16 (over y, z), blk: 8 (over x, core).
Axes of the slice: x: 4, y: 4, z: 4, core: 2. Of those that a mesh axis runs over, the one named last changes fastest.
Arguments:
- a_slots: bfloat16 [16, 8, 16, 2, 128, 128], P('grid', 'blk'), may hold values from -6 to 6
- a_rows: int32 [16, 8, 16, 2], P('grid', 'blk'), may hold values from 0 to 127, as said below
- a_cols: int32 [16, 8, 16, 2], P('grid', 'blk'), may hold values from 0 to 63
- a_count: int32 [16, 8, 16], P('grid', 'blk'), may hold values from 0 to 2, as said below
- owned_rows: int32 [16, 8], P('grid'), may hold values from 0 to 127, as said below
- b_matrix: bfloat16 [8192, 8192], P('grid', 'blk'), may hold values from -0.125 to 0.125
Outputs:
- product: bfloat16 [16384, 8192], P('grid', 'blk')
The draws below stay inside these ranges and needn't reach their ends.
Inputs may be any that keep to these rules, and one draw needn't show every extreme that they name: `a_rows`: every slot sent to product owner g, live or padded, names one of the block rows owned_rows[g, 0 .. 7]; no two slots of the whole draw name the same block row and block column. `a_count`: some product owner receives 2 live slots from every atom owner and atom column. `owned_rows`: A permutation of the 128 block rows.
All inputs are finite; a program needn't handle non-finite values.
Results may differ from the reference program's by a relative error of at most 0.001.
Values may be sent and summed in bfloat16 or wider, within the bound.
A program may use at most 128 MiB of HBM per device.

```python
import jax
import jax.numpy as jnp
from jax import lax

BS = 128
CAP = 2
RB = 8
KB = 4
NK = 64
NC = 64
N_GRID = 16
N_BLK = 8


def layout_tables(key):
    order = jax.random.permutation(jax.random.fold_in(key, 11), RB * N_GRID).astype(jnp.int32)
    owned = order.reshape(N_GRID, RB)
    place_keys = jax.random.split(jax.random.fold_in(key, 12), N_GRID)
    spots = jax.vmap(lambda one_key: jax.random.permutation(one_key, RB * KB * N_GRID))(place_keys)
    used = spots[:, :N_GRID * N_BLK * CAP].astype(jnp.int32)
    local_row = used // (KB * N_GRID)
    block_col = used % (KB * N_GRID)
    row_ids = jnp.take_along_axis(owned, local_row, axis=1)
    row_ids = row_ids.reshape(N_GRID, N_GRID, N_BLK, CAP).transpose(1, 2, 0, 3)
    col_ids = block_col.reshape(N_GRID, N_GRID, N_BLK, CAP).transpose(1, 2, 0, 3)
    counts = jax.random.randint(jax.random.fold_in(key, 13), (N_GRID, N_BLK, N_GRID), 0, CAP + 1)
    full_owner = jax.random.randint(jax.random.fold_in(key, 14), (), 0, N_GRID)
    owner_ids = jnp.arange(N_GRID)[None, None, :]
    counts = jnp.where(owner_ids == full_owner, CAP, counts)
    return (owned.astype(jnp.int32), row_ids.astype(jnp.int32), col_ids.astype(jnp.int32), counts.astype(jnp.int32))


def draw_a_rows(key, part):
    return layout_tables(key)[1]


def draw_a_cols(key, part):
    return layout_tables(key)[2]


def draw_a_count(key, part):
    return layout_tables(key)[3]


def draw_owned_rows(key, part):
    return layout_tables(key)[0]


def block_levels(own_key, shape, shards, least, top_value):
    def one(axis_at, shards_of):
        heights = jax.random.uniform(jax.random.fold_in(jax.random.fold_in(own_key, 6), axis_at), (shards_of,), jnp.float32, least / len(shards), top_value / len(shards))
        return jnp.repeat(jnp.exp(heights), shape[axis_at] // shards_of).reshape((-1,) + (1,) * (len(shape) - axis_at - 1))

    level = one(*shards[0])
    for cut in shards[1:]:
        level = level * one(*cut)
    return level


def centred(stream_key, dims, scale, bound, shards=(), kind=jnp.bfloat16):
    values = scale * jax.random.normal(stream_key, dims, jnp.float32)
    if shards:
        values = values * block_levels(stream_key, dims, shards, -0.22, 0.18)
    return jnp.clip(values, -bound, bound).astype(kind)


def setup_inputs(seed: int = 0) -> dict:
    seeds = jax.random.split(jax.random.key(seed), 7)
    a_slots = centred(seeds[0], (N_GRID, N_BLK, N_GRID, CAP, BS, BS), 1.0, 6.0, ((0, 16), (1, 8)))
    a_rows = draw_a_rows(jax.random.fold_in(seeds[6], 71), 0)
    a_cols = draw_a_cols(jax.random.fold_in(seeds[6], 71), 0)
    a_count = draw_a_count(jax.random.fold_in(seeds[6], 71), 0)
    owned_rows = draw_owned_rows(jax.random.fold_in(seeds[6], 71), 0)
    b_matrix = centred(seeds[5], (NK * BS, NC * BS), (KB * N_GRID * BS // 4) ** -0.5, 0.125, ((0, 16), (1, 8)))
    return {"a_slots": a_slots, "a_rows": a_rows, "a_cols": a_cols, "a_count": a_count, "owned_rows": owned_rows, "b_matrix": b_matrix}


def reference(a_slots, a_rows, a_cols, a_count, owned_rows, b_matrix):
    k_blocks = KB * N_GRID
    live = jnp.arange(CAP, dtype=jnp.int32)[None, None, None, :] < a_count[..., None]

    def one_owner(owner):
        data = jnp.take(a_slots, owner, axis=2).reshape(-1, BS, BS)
        slot_rows = jnp.take(a_rows, owner, axis=2).reshape(-1)
        slot_cols = jnp.take(a_cols, owner, axis=2).reshape(-1)
        alive = jnp.take(live, owner, axis=2).reshape(-1)
        owned = jnp.take(owned_rows, owner, axis=0)
        match = slot_rows[:, None] == owned[None, :]
        local_row = jnp.argmax(match, axis=1).astype(jnp.int32)
        keep = alive & jnp.any(match, axis=1)
        values = jnp.where(keep[:, None, None], data.astype(jnp.float32), jnp.float32(0.0))
        tile = jnp.zeros((RB, k_blocks, BS, BS), jnp.float32).at[local_row, slot_cols].add(values)
        tile = tile.astype(jnp.bfloat16).transpose(0, 2, 1, 3).reshape(RB * BS, k_blocks * BS)
        return jnp.dot(tile, b_matrix, preferred_element_type=jnp.float32).astype(jnp.bfloat16)

    blocks = lax.map(one_owner, jnp.arange(N_GRID, dtype=jnp.int32))
    return blocks.reshape(N_GRID * RB * BS, NC * BS)
```

```python
import jax
import jax.numpy as jnp
from jax import lax
from jax.experimental import pallas as pl
from jax.experimental.pallas import tpu as pltpu
from jax.sharding import PartitionSpec as P

CAP = 2
RB = 8
BS = 128
NY = 4
NZ = 4
NX = 4
NK = 64
NSLOT = 256
MESH = pl.DeviceIdType.MESH
F32 = jnp.float32
BF16 = jnp.bfloat16

HALF = 256
SUB = 128


def wrap(v):
    return lax.rem(v + 4, 4)


def build_labels():
    names = []
    for h in (0, 1):
        for s in (1, -1):
            names += [("m1", h, s), ("m2", h, s)]
            for j in (0, -1, 1):
                names += [("m3", h, j, s), ("m4", h, j, s)]
            names += [("m3a", h, s), ("m3b", h, s), ("m4", h, 2, s)]
    return {n: i for i, n in enumerate(names)}


LABELS = build_labels()
XLABELS = {n: i for i, n in enumerate(
    [(t, s) for s in (1, -1) for t in ("first", "second", "fwd", "meta")]
)}
CLABELS = {n: i for i, n in enumerate(["own", "xp1", "xp2", "xm1", "xm2", "far1", "far2", "mown", "mp", "mm", "mf"])}


def kernel(a_ref, rows_ref, cols_ref, cnt_ref, owned_ref, b_ref, o_ref,
           bpan, slots, tile, acc, outb, mine, mland, msm, idxv, idxs,
           bs, br, xs, xr, cs, cr, a1s, a1r, ms, mr, loc, oloc):
    g = lax.axis_index("grid")
    b = lax.axis_index("blk")
    y, z = g // NZ, lax.rem(g, NZ)
    x, c = b // 2, lax.rem(b, 2)

    def gid(dy, dz):
        return wrap(y + dy) * NZ + wrap(z + dz)

    def bid(dx):
        return wrap(x + dx) * 2 + c

    sib = x * 2 + (1 - c)

    code = rows_ref[...] * NK + cols_ref[...]
    cap_at = lax.broadcasted_iota(jnp.int32, (CAP, 16), 0)
    code = jnp.where(cap_at < cnt_ref[...], code, -1)
    mine[...] = jnp.full((CAP, 128), -1, jnp.int32)
    mine[:, 0:16] = code

    bar = pltpu.get_barrier_semaphore()

    @pl.loop(1, 16)
    def _(j):
        q = lax.rem(g + j, 16)
        pl.semaphore_signal(bar, 1, device_id=(q, b), device_id_type=MESH)

    for other in (bid(1), bid(-1), sib):
        pl.semaphore_signal(bar, 1, device_id=(g, other), device_id_type=MESH)
    pl.semaphore_wait(bar, 18)

    def start(src, dst, ssem, rsem, dev):
        pltpu.make_async_remote_copy(
            src_ref=src, dst_ref=dst, send_sem=ssem, recv_sem=rsem,
            device_id=dev, device_id_type=MESH).start()

    def arrive(ref, sem):
        pltpu.make_async_copy(ref, ref, sem).wait()

    def at(h, f, s):
        return gid(f, s) if h == 0 else gid(s, f)

    def region(h, f, s, part):
        lo = h * HALF + (SUB if part == "b" else 0)
        n = HALF if part == "ab" else SUB
        return bpan.at[at(h, f, s), pl.ds(lo, n)]

    def send(label, h, f, s, part, df, ds, own=False):
        i = LABELS[label]
        dst = region(h, f, s, part)
        if own:
            lo = h * HALF + (SUB if part == "b" else 0)
            n = HALF if part == "ab" else SUB
            src = b_ref.at[pl.ds(lo, n)]
        else:
            src = dst
        start(src, dst, bs.at[i], br.at[i], (at(h, df, ds), b))

    def got(label, h, f, s, part):
        arrive(region(h, f, s, part), br.at[LABELS[label]])

    SUBOF = {1: "a", -1: "b"}

    @pl.loop(1, 16)
    def _(j):
        q = lax.rem(g + j, 16)
        start(mine, mland.at[b * 16 + g], ms, mr, (q, b))

    @pl.loop(1, 16)
    def _(j):
        q = lax.rem(g + j, 16)
        start(a_ref.at[pl.ds(q * CAP, CAP)], slots.at[pl.ds(b * 32 + g * CAP, CAP)], a1s, a1r, (q, b))

    for h in (0, 1):
        for s in (1, -1):
            send(("m1", h, s), h, 0, 0, "ab", s, 0, own=True)
    for h in (0, 1):
        for s in (1, -1):
            send(("m3", h, 0, s), h, 0, 0, "ab", 0, s, own=True)
    own_b = pltpu.make_async_copy(b_ref, bpan.at[g], loc.at[0])
    own_b.start()
    own_a = pltpu.make_async_copy(a_ref.at[pl.ds(g * CAP, CAP)], slots.at[pl.ds(b * 32 + g * CAP, CAP)], loc.at[1])
    own_a.start()
    own_m = pltpu.make_async_copy(mine, mland.at[b * 16 + g], loc.at[2])
    own_m.start()
    own_a.wait()
    own_m.wait()
    arrive(slots.at[pl.ds(0, 30)], a1r)
    arrive(mland.at[pl.ds(0, 15)], mr)

    def srow(bb, part):
        if part == "all":
            return slots.at[pl.ds(bb * 32, 32)]
        return slots.at[pl.ds(bb * 32 + (16 if part == "b" else 0), 16)]

    def mrow(bb):
        return mland.at[pl.ds(bb * 16, 16)]

    def xsend(label, ref, s):
        i = XLABELS[(label, s)]
        start(ref, ref, xs.at[i], xr.at[i], (g, bid(s)))

    def xgot(label, ref, s):
        arrive(ref, xr.at[XLABELS[(label, s)]])

    def csend(label, ref):
        i = CLABELS[label]
        start(ref, ref, cs.at[i], cr.at[i], (g, sib))

    def cgot(label, ref):
        arrive(ref, cr.at[CLABELS[label]])

    for s in (1, -1):
        xsend("meta", mrow(b), s)
        xsend("first", srow(b, "a" if s == 1 else "b"), s)
        xsend("second", srow(b, "b" if s == 1 else "a"), s)
    csend("own", srow(b, "all"))
    csend("mown", mrow(b))

    for h in (0, 1):
        for s in (1, -1):
            got(("m1", h, s), h, -s, 0, "ab")
            send(("m2", h, s), h, -s, 0, SUBOF[s], s, 0)
    for h in (0, 1):
        for j in (-1, 1):
            for s in (1, -1):
                send(("m3", h, j, s), h, j, 0, "ab", 0, s)

    for s in (1, -1):
        xgot("meta", mrow(bid(-s)), s)
        csend("mp" if s == 1 else "mm", mrow(bid(-s)))
        if s == 1:
            start(mrow(bid(-1)), mrow(bid(-1)), loc.at[3], loc.at[4], (g, bid(1)))
        xgot("first", srow(bid(-s), "a" if s == 1 else "b"), s)
        xsend("fwd", srow(bid(-s), "a" if s == 1 else "b"), s)
        csend("xp1" if s == 1 else "xm1", srow(bid(-s), "a" if s == 1 else "b"))

    for h in (0, 1):
        for s in (1, -1):
            got(("m3", h, 0, s), h, 0, -s, "ab")
            send(("m4", h, 0, s), h, 0, -s, SUBOF[s], 0, s)
    for h in (0, 1):
        got(("m2", h, 1), h, 2, 0, "a")
        for s in (1, -1):
            send(("m3a", h, s), h, 2, 0, "a", 0, s)
        got(("m2", h, -1), h, 2, 0, "b")
        for s in (1, -1):
            send(("m3b", h, s), h, 2, 0, "b", 0, s)

    for s in (1, -1):
        xgot("second", srow(bid(-s), "b" if s == 1 else "a"), s)
        csend("xp2" if s == 1 else "xm2", srow(bid(-s), "b" if s == 1 else "a"))
    arrive(mrow(bid(2)), loc.at[4])
    csend("mf", mrow(bid(2)))
    xgot("fwd", srow(bid(2), "a"), 1)
    csend("far1", srow(bid(2), "a"))
    xgot("fwd", srow(bid(2), "b"), -1)
    csend("far2", srow(bid(2), "b"))

    def sb(dx):
        return wrap(x + dx) * 2 + (1 - c)

    cgot("mown", mrow(sb(0)))
    cgot("mp", mrow(sb(-1)))
    cgot("mm", mrow(sb(1)))
    cgot("mf", mrow(sb(2)))

    meta_copy = pltpu.make_async_copy(mland, msm, loc.at[5])
    meta_copy.start()
    meta_copy.wait()
    sub_at = lax.broadcasted_iota(jnp.int32, (RB, 128), 0)
    lane_at = lax.broadcasted_iota(jnp.int32, (RB, 128), 1)
    want = lane_at
    for i in range(RB):
        want = jnp.where(sub_at == i, owned_ref[0, i] * NK + lane_at, want)
    want = jnp.where(lane_at < NK, want, -2)

    def find(r, where):
        for cap in range(CAP):
            where = jnp.where(want == msm[r, cap, g], r * CAP + cap, where)
        return where

    idxv[...] = lax.fori_loop(0, NSLOT // CAP, find, jnp.full((RB, 128), -1, jnp.int32))
    idx_copy = pltpu.make_async_copy(idxv, idxs, loc.at[6])
    idx_copy.start()
    idx_copy.wait()

    cgot("own", srow(sb(0), "all"))
    cgot("xp1", srow(sb(-1), "a"))
    cgot("xm1", srow(sb(1), "b"))
    cgot("xp2", srow(sb(-1), "b"))
    cgot("xm2", srow(sb(1), "a"))
    cgot("far1", srow(sb(2), "a"))
    cgot("far2", srow(sb(2), "b"))

    @pl.loop(0, 16)
    def _(p):
        for kk in range(4):
            for i in range(RB):
                s = idxs[i, p * 4 + kk]
                data = slots[jnp.maximum(s, 0)]
                tile[p, i * BS:(i + 1) * BS, kk * BS:(kk + 1) * BS] = jnp.where(s >= 0, data, jnp.zeros_like(data))

    def mm(p, lo, n, first=False):
        @pl.loop(0, 4)
        def _(t):
            col = pl.ds(pl.multiple_of(t * 256, 256), 256)
            part = jnp.dot(tile[p, :, lo:lo + n], bpan[p, lo:lo + n, col], preferred_element_type=F32)
            if first:
                acc[:, col] = part
            else:
                acc[:, col] += part

    own_b.wait()
    mm(gid(0, 0), 0, 512, first=True)
    for h, j in ((0, -1), (1, -1), (0, 1), (1, 1)):
        mm(at(h, j, 0), 0, 512)

    for h in (0, 1):
        for j in (-1, 1):
            for s in (1, -1):
                got(("m3", h, j, s), h, j, -s, "ab")
                send(("m4", h, j, s), h, j, -s, SUBOF[s], 0, s)
    for dy in (-1, 1):
        for dz in (-1, 1):
            mm(gid(dy, dz), 0, 512)

    for h in (0, 1):
        for s in (1, -1):
            got(("m3a", h, s), h, 2, -s, "a")
            got(("m3b", h, s), h, 2, -s, "b")
            send(("m4", h, 2, s), h, 2, -s, SUBOF[s], 0, s)
    for h in (0, 1):
        got(("m4", h, 0, 1), h, 0, 2, "a")
        got(("m4", h, 0, -1), h, 0, 2, "b")
    mm(gid(2, 0), 0, 512)
    mm(gid(0, 2), 0, 512)
    for h in (0, 1):
        for j in (-1, 1):
            got(("m4", h, j, 1), h, j, 2, "a")
            got(("m4", h, j, -1), h, j, 2, "b")
    for d in (-1, 1):
        mm(gid(2, d), 0, 512)
        mm(gid(d, 2), 0, 512)
    for h in (0, 1):
        got(("m4", h, 2, 1), h, 2, 2, "a")
        got(("m4", h, 2, -1), h, 2, 2, "b")

    last = gid(2, 2)
    for t in range(4):
        col = pl.ds(t * 256, 256)
        part = jnp.dot(tile[last], bpan[last, :, col], preferred_element_type=F32)
        outb[:, col] = (acc[:, col] + part).astype(BF16)
        pltpu.make_async_copy(outb.at[:, col], o_ref.at[:, col], oloc.at[t]).start()
    for t in range(4):
        col = pl.ds(t * 256, 256)
        pltpu.make_async_copy(outb.at[:, col], o_ref.at[:, col], oloc.at[t]).wait()

    arrive(slots.at[pl.ds(0, 30)], a1s)
    arrive(mland.at[pl.ds(0, 15)], ms)
    arrive(mrow(b), loc.at[3])
    for name, i in LABELS.items():
        n = HALF if name[0] in ("m1", "m3") else SUB
        arrive(bpan.at[0, pl.ds(0, n)], bs.at[i])
    for (t, s), i in XLABELS.items():
        arrive(mrow(b) if t == "meta" else srow(b, "a"), xs.at[i])
    for t, i in CLABELS.items():
        arrive(mrow(b) if t[0] == "m" else srow(b, "all" if t == "own" else "a"), cs.at[i])


def body(a_slots, a_rows, a_cols, a_count, owned_rows, b_matrix):
    DMA = pltpu.SemaphoreType.DMA
    any_space = pl.BlockSpec(memory_space=pl.ANY)
    vmem = pl.BlockSpec(memory_space=pltpu.VMEM)
    smem = pl.BlockSpec(memory_space=pltpu.SMEM)
    return pl.pallas_call(
        kernel,
        out_shape=jax.ShapeDtypeStruct((RB * BS, b_matrix.shape[1]), BF16),
        in_specs=[any_space, vmem, vmem, vmem, smem, any_space],
        out_specs=any_space,
        scratch_shapes=[
            pltpu.VMEM((16, 512, 1024), BF16),
            pltpu.VMEM((NSLOT, BS, BS), BF16),
            pltpu.VMEM((16, RB * BS, 512), BF16),
            pltpu.VMEM((RB * BS, 1024), F32),
            pltpu.VMEM((RB * BS, 1024), BF16),
            pltpu.VMEM((CAP, 128), jnp.int32),
            pltpu.VMEM((128, CAP, 128), jnp.int32),
            pltpu.SMEM((128, CAP, 128), jnp.int32),
            pltpu.VMEM((RB, 128), jnp.int32),
            pltpu.SMEM((RB, 128), jnp.int32),
            DMA((len(LABELS),)), DMA((len(LABELS),)),
            DMA((len(XLABELS),)), DMA((len(XLABELS),)),
            DMA((len(CLABELS),)), DMA((len(CLABELS),)),
            DMA, DMA, DMA, DMA, DMA((7,)), DMA((4,)),
        ],
        compiler_params=pltpu.CompilerParams(
            collective_id=0, has_side_effects=True, vmem_limit_bytes=60 << 20),
    )(
        a_slots.reshape(16 * CAP, BS, BS),
        a_rows.reshape(16, CAP).T,
        a_cols.reshape(16, CAP).T,
        a_count.reshape(1, 16),
        owned_rows,
        b_matrix,
    )


def solution(mesh):
    in_specs = (
        P("grid", "blk", None, None, None, None),
        P("grid", "blk", None, None),
        P("grid", "blk", None, None),
        P("grid", "blk", None),
        P("grid", None),
        P("grid", "blk"),
    )
    return jax.shard_map(body, mesh=mesh, in_specs=in_specs, out_specs=P("grid", "blk"), check_vma=False)
```

```python
import jax
import jax.numpy as jnp
from jax import lax
from jax.experimental import pallas as pl
from jax.experimental.pallas import tpu as pltpu
from jax.sharding import PartitionSpec as P

CAP = 2
RB = 8
BS = 128
NZ = 4
NK = 64
WIDTH = (256, 256)
LEFT = (0, 256)
CH = 16
SF = 12
R1 = 288
ROWS = 512
NONE = 256
PIECES = ((0, 0), (0, 1), (0, 3), (1, 0), (0, 2), (1, 1), (1, 3), (1, 2))
MESH = pl.DeviceIdType.MESH
F32 = jnp.float32
BF16 = jnp.bfloat16


def wrap(v):
    return lax.rem(v + 4, 4)


class Labels:
    def __init__(self, names):
        self.at = {n: i for i, n in enumerate(names)}

    def __len__(self):
        return len(self.at)


B_LABELS = Labels(
    [(n, k) for n in (0, 1) for k in ("cross", "w1", "w2own", "w2a", "w2b")]
    + [(n, k, s) for n in (0, 1) for s in (1, -1)
       for k in ("z1own", "z1far", "z2own", "z2far", "y1own", "y2own", "w2")]
)
X_LABELS = Labels(
    [(k, i, t, s) for k in (0, 1) for i in "OQ" for t in ("full", "fwd") for s in (1, -1)
     if (k, i, t) not in ((0, "O", "full"), (1, "O", "full"))]
    + [(1, "O", t, s) for t in ("fulla", "fullb") for s in (1, -1)]
    + [("piece", j, s) for j in range(8) for s in (1, -1)]
    + [("meta", 1), ("meta", -1), ("metafwd", 1)]
)
P_LABELS = Labels([("pa", k) for k in (0, 1)] + [("pf", d) for d in (0, 1, -1, 2)])
C_LABELS = Labels(
    [(k, i, t) for k in (0, 1) for i in "OQ" for t in ("own", "xp", "xm", "fp", "fm")]
    + [("pf", d) for d in (0, 1, -1, 2)]
    + ["m0", "mp", "mm", "mf"]
)


def kernel(a_ref, rows_ref, cols_ref, cnt_ref, owned_ref, b_ref, o_ref,
           bp0, bp1, bx0, bx1, slots0, slots1, accp0, accp1, acco0, acco1, outp0, outp1, mine, mland, msm, idxv, idxs,
           bs, br, xs, xr, ps, pr, cs, cr, a1s, a1r, ms, mr, loc, outs, outr):
    g = lax.axis_index("grid")
    b = lax.axis_index("blk")
    y, z = g // NZ, lax.rem(g, NZ)
    x, c = b // 2, lax.rem(b, 2)

    def side(yv):
        return lax.rem((yv + 1) // 2, 2)

    def partner(yv):
        return yv + 1 - 2 * lax.rem(yv, 2)

    def order(yv, zv):
        return side(yv) * 8 + (yv // 2) * 4 + zv

    s = side(y)
    t = 1 - s
    gp = partner(y) * NZ + z
    gcls = (gp, g)
    pair = (gp, b)
    across = ((3 - y) * NZ + z, b)
    sib = x * 2 + (1 - c)

    def bid(dx):
        return wrap(x + dx) * 2 + c

    def sb(dx):
        return wrap(x + dx) * 2 + (1 - c)

    def zdev(d):
        return (y * NZ + wrap(z + d), b)

    slots = (slots0, slots1)
    bp, bx, outp = (bp0, bp1), (bx0, bx1), (outp0, outp1)
    accs = ((accp0, accp1), (acco0, acco1))

    code = rows_ref[...] * NK + cols_ref[...]
    cap_at = lax.broadcasted_iota(jnp.int32, (CAP, 16), 0)
    code = jnp.where(cap_at < cnt_ref[...], code, -1)
    mine[...] = jnp.full((1, 128), -1, jnp.int32)
    for cap in range(CAP):
        mine[:, cap * 16:cap * 16 + 16] = code[cap:cap + 1]
    mine[:, 32:32 + RB] = owned_ref[...]
    for k in (0, 1):
        slots[k][NONE] = jnp.zeros((BS, BS), BF16)

    bar = pltpu.get_barrier_semaphore()

    @pl.loop(1, 16)
    def _(j):
        q = lax.rem(g + j, 16)
        pl.semaphore_signal(bar, 1, device_id=(q, b), device_id_type=MESH)

    for other in (bid(1), bid(-1), sib):
        pl.semaphore_signal(bar, 1, device_id=(g, other), device_id_type=MESH)
    pl.semaphore_wait(bar, 18)

    def start(src, dst, ssem, rsem, dev):
        pltpu.make_async_remote_copy(
            src_ref=src, dst_ref=dst, send_sem=ssem, recv_sem=rsem,
            device_id=dev, device_id_type=MESH).start()

    def arrive(ref, sem):
        pltpu.make_async_copy(ref, ref, sem).wait()

    def k0(yv, zv):
        return (yv // 2) * 8 + zv * 2

    def breg(n, yv, zv, part):
        lo, cnt = {
            "w": (0, R1), "wa": (0, R1 // 2), "wb": (R1 // 2, R1 // 2),
            "z": (R1, ROWS - R1), "za": (R1, (ROWS - R1) // 2),
            "zb": (R1 + (ROWS - R1) // 2, (ROWS - R1) // 2),
        }[part]
        return bp[n].at[pl.ds(k0(yv, zv), 2), pl.ds(lo, cnt)]

    def chunk(k, b0, s0, lo=0, n=CH):
        return slots[k].at[pl.ds(b0 * 32 + s0 * CH + lo, n)]

    def bsend(label, ref, dev):
        i = B_LABELS.at[label]
        start(ref, ref, bs.at[i], br.at[i], dev)

    def bgot(label, ref):
        arrive(ref, br.at[B_LABELS.at[label]])

    def xsend(label, ref, d):
        i = X_LABELS.at[label]
        start(ref, ref, xs.at[i], xr.at[i], (g, bid(d)))

    def xgot(label, ref):
        arrive(ref, xr.at[X_LABELS.at[label]])

    def psend(label, k, *where):
        i = P_LABELS.at[label]
        start(chunk(k, *where), chunk(1 - k, *where), ps.at[i], pr.at[i], pair)

    def pgot(label, ref):
        arrive(ref, pr.at[P_LABELS.at[label]])

    def csend(label, ref):
        i = C_LABELS.at[label]
        start(ref, ref, cs.at[i], cr.at[i], (g, sib))

    def cgot(label, ref):
        arrive(ref, cr.at[C_LABELS.at[label]])

    here = order(y, z) * CAP

    def a_dst(k):
        return slots[k].at[pl.ds(b * 32 + here, CAP)]

    def a_send(k):
        for j, (far, dz) in enumerate(PIECES):
            yv, zv = (3 - y if far else y), wrap(z + dz)
            owner = (partner(yv) if k == 0 else yv) * NZ + zv
            src = a_ref.at[pl.ds(owner * CAP, CAP)]
            rsem = a1r.at[j] if k == 0 else a1r.at[8]
            if j == 0:
                pltpu.make_async_copy(src, a_dst(k), loc.at[6 + k]).start()
            else:
                start(src, a_dst(k), a1s.at[k], rsem, (yv * NZ + zv, b))

    def piece(j, b0):
        far, dz = PIECES[j]
        at = order(3 - y if far else y, wrap(z - dz)) * CAP
        return slots0.at[pl.ds(b0 * 32 + at, CAP)]

    def x_pieces(js):
        for j in js:
            arrive(piece(j, b), loc.at[6] if j == 0 else a1r.at[j])
            for d in (1, -1):
                xsend(("piece", j, d), piece(j, b), d)

    kown = k0(y, z) + lax.rem(y, 2)

    def b_cols(side_at, n):
        return pl.ds(pl.multiple_of(side_at * 512 + LEFT[n], 128), WIDTH[n])

    a_send(0)
    own_b, cross_b = [], []
    for n in (0, 1):
        cp = pltpu.make_async_copy(b_ref.at[:, b_cols(t, n)], bx[n], loc.at[n])
        cp.start()
        cross_b.append(cp)
    for n in (0, 1):
        cp = pltpu.make_async_copy(b_ref.at[:, b_cols(s, n)], bp[n].at[kown], loc.at[2 + n])
        cp.start()
        own_b.append(cp)
    for n in (0, 1):
        cross_b[n].wait()
        i = B_LABELS.at[(n, "cross")]
        start(bx[n], bp[n].at[kown], bs.at[i], br.at[i], pair)

    @pl.loop(1, 16)
    def _(j):
        q = lax.rem(g + j, 16)
        start(mine, mland.at[b * 16 + g], ms, mr, (q, b))

    pltpu.make_async_copy(mine, mland.at[b * 16 + g], loc.at[8]).start()

    kpair = k0(y, z) + 1 - lax.rem(y, 2)

    def b_start(n):
        own_b[n].wait()
        bgot((n, "cross"), bp[n].at[kpair])
        bsend((n, "w1"), breg(n, y, z, "w"), across)
        for d in (1, -1):
            bsend((n, "z1own", d), breg(n, y, z, "w"), zdev(d))
        for d in (1, -1):
            bsend((n, "y1own", d), breg(n, y, z, "z"), zdev(d))
        bsend((n, "w2own"), breg(n, y, z, "z"), across)

    HALF = {1: "a", -1: "b"}

    def b_step1(n):
        bgot((n, "w1"), breg(n, 3 - y, z, "w"))
        for d in (1, -1):
            bsend((n, "z1far", d), breg(n, 3 - y, z, "w"), zdev(d))
        for d in (1, -1):
            bgot((n, "z1own", d), breg(n, y, wrap(z - d), "w"))
            bsend((n, "z2own", d), breg(n, y, wrap(z - d), "w" + HALF[d]), zdev(d))

    def b_step2(n):
        for d in (1, -1):
            bgot((n, "y1own", d), breg(n, y, wrap(z - d), "z"))
            bsend((n, "w2", d), breg(n, y, wrap(z - d), "z"), across)
            bsend((n, "y2own", d), breg(n, y, wrap(z - d), "z" + HALF[d]), zdev(d))

    def b_step3(n):
        for d in (1, -1):
            bgot((n, "z1far", d), breg(n, 3 - y, wrap(z - d), "w"))
            bsend((n, "z2far", d), breg(n, 3 - y, wrap(z - d), "w" + HALF[d]), zdev(d))
        for d in (1, -1):
            bgot((n, "y2own", d), breg(n, y, wrap(z + 2), "z" + HALF[d]))
            bsend((n, "w2" + HALF[d]), breg(n, y, wrap(z + 2), "z" + HALF[d]), across)

    def b_got_q(n, q):
        if q == 0:
            bgot((n, "w2own"), breg(n, 3 - y, z, "z"))
        elif q < 3:
            d = -1 if q == 1 else 1
            bgot((n, "w2", d), breg(n, 3 - y, wrap(z - d), "z"))
        else:
            for d in (1, -1):
                bgot((n, "z2own", d), breg(n, y, wrap(z + 2), "w" + HALF[d]))
                bgot((n, "z2far", d), breg(n, 3 - y, wrap(z + 2), "w" + HALF[d]))
                bgot((n, "w2" + HALF[d]), breg(n, 3 - y, wrap(z + 2), "z" + HALF[d]))

    def item(k, i, b0, part="all"):
        s0, n = (s, CH) if i == "O" else (t, SF if k == 1 else CH)
        h = n // 2
        lo, cnt = {"all": (0, n), "a": (0, h), "b": (h, n - h)}[part]
        return chunk(k, b0, s0, lo, cnt)

    def x_full(k, i):
        for d in (1, -1):
            xsend((k, i, "full", d), item(k, i, b), d)
        csend((k, i, "own"), item(k, i, b))

    def x_part(part):
        for d in (1, -1):
            xsend((1, "O", "full" + part, d), item(1, "O", b, part), d)

    def x_fwd(k, i):
        for d in (1, -1):
            if (k, i) == (0, "O"):
                for j in range(8):
                    xgot(("piece", j, d), piece(j, bid(-d)))
            elif (k, i) == (1, "O"):
                for part in "ab":
                    xgot((k, i, "full" + part, d), item(k, i, bid(-d), part))
            else:
                xgot((k, i, "full", d), item(k, i, bid(-d)))
            xsend((k, i, "fwd", d), item(k, i, bid(-d), HALF[d]), d)
            csend((k, i, "xp" if d == 1 else "xm"), item(k, i, bid(-d)))

    def x_last(k, i):
        for d in (1, -1):
            xgot((k, i, "fwd", d), item(k, i, bid(2), HALF[d]))
            csend((k, i, "fp" if d == 1 else "fm"), item(k, i, bid(2), HALF[d]))

    def c_end(k, i):
        cgot((k, i, "own"), item(k, i, sb(0)))
        cgot((k, i, "xp"), item(k, i, sb(-1)))
        cgot((k, i, "xm"), item(k, i, sb(1)))
        cgot((k, i, "fp"), item(k, i, sb(2), "a"))
        cgot((k, i, "fm"), item(k, i, sb(2), "b"))

    def p_rest():
        for d in (0, 1, -1, 2):
            psend(("pf", d), 0, bid(d), s, SF, CH - SF)

    def p_rest_got():
        for d in (0, 1, -1, 2):
            ref = chunk(1, bid(d), t, SF, CH - SF)
            pgot(("pf", d), ref)
            csend(("pf", d), ref)

    def c_rest_end():
        for d in (0, 1, -1, 2):
            cgot(("pf", d), chunk(1, sb(d), t, SF, CH - SF))

    def mrow(bb):
        return mland.at[pl.ds(bb * 16, 16)]

    def meta_start():
        pltpu.make_async_copy(mland, msm, loc.at[4]).start()

    def find_all():
        pltpu.make_async_copy(mland, msm, loc.at[4]).wait()
        sub_at = lax.broadcasted_iota(jnp.int32, (RB, 128), 0)
        lane_at = lax.broadcasted_iota(jnp.int32, (RB, 128), 1)
        wants = []
        for k in (0, 1):
            want = lane_at
            for i in range(RB):
                want = jnp.where(sub_at == i, msm[b * 16 + gcls[k], 0, 32 + i] * NK + lane_at, want)
            wants.append(jnp.where(lane_at < NK, want, -2))

        def find(b0, where):
            out = []
            for k in (0, 1):
                w = where[k]
                base = b0 * 32
                for g0 in range(16):
                    yv, zv = g0 // NZ, g0 % NZ
                    at = (((yv + 1) // 2) % 2 * 8 + (yv // 2) * 4 + zv) * CAP
                    for cap in range(CAP):
                        w = jnp.where(wants[k] == msm[b0 * 16 + g0, 0, cap * 16 + gcls[k]], base + at + cap, w)
                out.append(w)
            return tuple(out)

        none = jnp.full((RB, 128), NONE, jnp.int32)
        found = lax.fori_loop(0, 8, find, (none, none))
        for k in (0, 1):
            idxv[k] = found[k]
        idx_copy = pltpu.make_async_copy(idxv, idxs, loc.at[5])
        idx_copy.start()
        idx_copy.wait()

    DZ = (0, 1, -1, 2)

    def dot(k, n, q, rows=(0, RB)):
        zv = wrap(z + DZ[q])
        kbs = [k0(y, zv), k0(y, zv) + 1, k0(3 - y, zv), k0(3 - y, zv) + 1]
        lhs = []
        for i in range(*rows):
            blocks = []
            for kb in kbs:
                gb = ((kb // 8) * 2 + lax.rem(kb, 2)) * NZ + lax.rem(kb, 8) // 2
                blocks += [slots[k][idxs[k, i, gb * 4 + kk]] for kk in range(4)]
            lhs.append(jnp.concatenate(blocks, axis=1))
        rhs = jnp.concatenate(
            [bp[n][pl.ds(kb, 2)].reshape(2 * ROWS, WIDTH[n]) for kb in (kbs[0], kbs[2])], axis=0)
        return jnp.dot(jnp.concatenate(lhs, axis=0), rhs, preferred_element_type=F32)

    def add(k, n, q, rows=(0, RB)):
        lo, hi = rows[0] * BS, rows[1] * BS
        part = dot(k, n, q, rows)
        acc = accs[k][n]
        if q == 0:
            acc[lo:hi] = part
        elif q < 3:
            acc[lo:hi] += part
        elif k == 0:
            outp[n][lo:hi] = (acc[lo:hi] + part).astype(BF16)
        else:
            o_ref[lo:hi, b_cols(s, n)] = (acc[lo:hi] + part).astype(BF16)

    SWAPS = ((0, 0, 8), (1, 0, 4), (1, 4, 8))

    def swap(j):
        n, lo, hi = SWAPS[j]
        add(0, n, 3, (lo, hi))
        rows = pl.ds(lo * BS, (hi - lo) * BS)
        start(outp[n].at[rows], o_ref.at[rows, b_cols(s, n)], outs.at[j], outr.at[j], pair)

    x_pieces((0, 1, 2, 3))
    a_send(1)
    x_pieces((4, 5, 6, 7))
    csend((0, "O", "own"), item(0, "O", b))
    b_start(0)
    arrive(a_dst(1), loc.at[7])
    arrive(slots1.at[pl.ds(0, 14)], a1r.at[8])
    for k in (1, 0):
        psend(("pa", k), k, b, s, 0, SF if k == 0 else CH)
    csend((1, "O", "own"), item(1, "O", b))
    x_fwd(0, "O")
    x_part("a")
    arrive(mland.at[b * 16 + g], loc.at[8])
    arrive(mland.at[pl.ds(0, 15)], mr)
    for d in (1, -1):
        xsend(("meta", d), mrow(b), d)
    csend("m0", mrow(b))
    b_step1(0)
    x_last(0, "O")
    p_rest()
    pgot(("pa", 1), item(0, "Q", b))
    x_full(0, "Q")
    b_step2(0)
    b_start(1)
    for d in (1, -1):
        xgot(("meta", d), mrow(bid(-d)))
        csend("mp" if d == 1 else "mm", mrow(bid(-d)))
    xsend(("metafwd", 1), mrow(bid(-1)), 1)
    b_step3(0)
    x_fwd(0, "Q")
    x_part("b")
    xgot(("metafwd", 1), mrow(bid(2)))
    csend("mf", mrow(bid(2)))
    cgot("m0", mrow(sb(0)))
    cgot("mp", mrow(sb(-1)))
    cgot("mm", mrow(sb(1)))
    cgot("mf", mrow(sb(2)))
    meta_start()
    pgot(("pa", 0), item(1, "Q", b))
    x_full(1, "Q")
    find_all()
    x_last(0, "Q")
    for i in "OQ":
        c_end(0, i)
    b_got_q(0, 0)
    add(0, 0, 0)
    b_got_q(0, 1)
    add(0, 0, 1)
    b_step1(1)
    b_got_q(0, 2)
    add(0, 0, 2)
    b_got_q(0, 3)
    swap(0)
    x_fwd(1, "O")
    b_step2(1)
    p_rest_got()
    x_fwd(1, "Q")
    x_last(1, "O")
    b_step3(1)
    for q in range(3):
        b_got_q(1, q)
        add(0, 1, q)
    x_last(1, "Q")
    b_got_q(1, 3)
    swap(1)
    swap(2)
    for i in "OQ":
        c_end(1, i)
    c_rest_end()
    for n in (0, 1):
        for q in range(4):
            add(1, n, q)

    for j, (n, lo, hi) in enumerate(SWAPS):
        arrive(o_ref.at[pl.ds(lo * BS, (hi - lo) * BS), b_cols(t, n)], outr.at[j])

    for k in (0, 1):
        arrive(slots[k].at[pl.ds(0, 14)], a1s.at[k])
    arrive(mland.at[pl.ds(0, 15)], ms)
    sizes = {"cross": "x", "w1": "w", "z1own": "w", "z1far": "w", "z2own": "wa", "z2far": "wa",
             "y1own": "z", "y2own": "za", "w2own": "z", "w2": "z", "w2a": "za", "w2b": "zb"}
    for name, i in B_LABELS.at.items():
        part = sizes[name[1]]
        arrive(bx[name[0]] if part == "x" else breg(name[0], 0, 0, part), bs.at[i])
    for name, i in X_LABELS.at.items():
        if name[0] in ("meta", "metafwd"):
            arrive(mrow(b), xs.at[i])
        elif name[0] == "piece":
            arrive(piece(0, b), xs.at[i])
        else:
            k, it, kind, d = name
            arrive(item(k, it, b, {"full": "all", "fwd": HALF[d]}.get(kind, kind[-1])), xs.at[i])
    for name, i in P_LABELS.at.items():
        arrive(chunk(0, 0, 0, 0, {("pa", 0): SF, ("pa", 1): CH}.get(name, CH - SF)), ps.at[i])
    for name, i in C_LABELS.at.items():
        if isinstance(name, str):
            arrive(mrow(b), cs.at[i])
        elif name[0] == "pf":
            arrive(chunk(0, 0, 0, 0, CH - SF), cs.at[i])
        else:
            part = {"own": "all", "xp": "all", "xm": "all", "fp": "a", "fm": "b"}[name[2]]
            arrive(item(name[0], name[1], b, part), cs.at[i])
    for j, (n, lo, hi) in enumerate(SWAPS):
        arrive(outp[n].at[pl.ds(lo * BS, (hi - lo) * BS)], outs.at[j])


def body(a_slots, a_rows, a_cols, a_count, owned_rows, b_matrix):
    DMA = pltpu.SemaphoreType.DMA
    any_space = pl.BlockSpec(memory_space=pl.ANY)
    vmem = pl.BlockSpec(memory_space=pltpu.VMEM)
    return pl.pallas_call(
        kernel,
        out_shape=pltpu.VMEM((RB * BS, b_matrix.shape[1]), BF16),
        in_specs=[any_space, vmem, vmem, vmem, vmem, any_space],
        out_specs=vmem,
        scratch_shapes=[
            *[pltpu.VMEM((16, ROWS, w), BF16) for w in WIDTH],
            *[pltpu.VMEM((ROWS, w), BF16) for w in WIDTH],
            pltpu.VMEM((NONE + 1, BS, BS), BF16),
            pltpu.VMEM((NONE + 1, BS, BS), BF16),
            *[pltpu.VMEM((RB * BS, w), F32) for w in WIDTH * 2],
            *[pltpu.VMEM((RB * BS, w), BF16) for w in WIDTH],
            pltpu.VMEM((1, 128), jnp.int32),
            pltpu.VMEM((128, 1, 128), jnp.int32),
            pltpu.SMEM((128, 1, 128), jnp.int32),
            pltpu.VMEM((2, RB, 128), jnp.int32),
            pltpu.SMEM((2, RB, 128), jnp.int32),
            DMA((len(B_LABELS),)), DMA((len(B_LABELS),)),
            DMA((len(X_LABELS),)), DMA((len(X_LABELS),)),
            DMA((len(P_LABELS),)), DMA((len(P_LABELS),)),
            DMA((len(C_LABELS),)), DMA((len(C_LABELS),)),
            DMA((2,)), DMA((9,)), DMA, DMA, DMA((9,)), DMA((3,)), DMA((3,)),
        ],
        compiler_params=pltpu.CompilerParams(
            collective_id=0, has_side_effects=True, vmem_limit_bytes=60 << 20),
    )(
        a_slots.reshape(16 * CAP, BS, BS),
        a_rows.reshape(16, CAP).T,
        a_cols.reshape(16, CAP).T,
        a_count.reshape(1, 16),
        owned_rows,
        b_matrix,
    )


def solution(mesh):
    in_specs = (
        P("grid", "blk", None, None, None, None),
        P("grid", "blk", None, None),
        P("grid", "blk", None, None),
        P("grid", "blk", None),
        P("grid", None),
        P("grid", "blk"),
    )
    return jax.shard_map(body, mesh=mesh, in_specs=in_specs, out_specs=P("grid", "blk"), check_vma=False)
```

```python
import jax
import jax.numpy as jnp
from jax import lax
from jax.experimental import pallas as pl
from jax.experimental.pallas import tpu as pltpu
from jax.sharding import PartitionSpec as P

CAP = 2
RB = 8
BS = 128
NZ = 4
NK = 64
WIDTH = (256, 256)
LEFT = (0, 256)
CH = 16
SF = 10
R1 = 288
ROWS = 512
NONE = 256
PIECES = ((0, 0), (0, 1), (0, 3), (1, 0), (0, 2), (1, 1), (1, 3), (1, 2))
MESH = pl.DeviceIdType.MESH
F32 = jnp.float32
BF16 = jnp.bfloat16


def wrap(v):
    return lax.rem(v + 4, 4)


class Labels:
    def __init__(self, names):
        self.at = {n: i for i, n in enumerate(names)}

    def __len__(self):
        return len(self.at)


B_LABELS = Labels(
    [(n, k) for n in (0, 1) for k in ("cross", "w1", "w2own", "w2a", "w2b")]
    + [(n, k, s) for n in (0, 1) for s in (1, -1)
       for k in ("z1own", "z1far", "z2own", "z2far", "y1own", "y2own", "w2")]
)
X_LABELS = Labels(
    [(k, i, t, s) for k in (0, 1) for i in "OQ" for t in ("full", "fwd") for s in (1, -1)
     if (k, i, t) not in ((0, "O", "full"), (1, "O", "full"))]
    + [(1, "O", t, s) for t in ("fulla", "fullb") for s in (1, -1)]
    + [("piece", j, s) for j in range(8) for s in (1, -1)]
    + [("meta", 1), ("meta", -1), ("metafwd", 1)]
)
P_LABELS = Labels([("pa", k) for k in (0, 1)] + [("pf", d) for d in (0, 1, -1, 2)])
C_LABELS = Labels(
    [(k, i, t) for k in (0, 1) for i in "OQ" for t in ("own", "xp", "xm", "fp", "fm")]
    + [("pf", d) for d in (0, 1, -1, 2)]
    + ["m0", "mp", "mm", "mf"]
)


def kernel(a_ref, rows_ref, cols_ref, cnt_ref, owned_ref, b_ref, o_ref,
           bp0, bp1, bx0, bx1, slots0, slots1, accp0, accp1, acco0, acco1, outp0, outp1, mine, mland, msm, idxv, idxs,
           bs, br, xs, xr, ps, pr, cs, cr, a1s, a1r, ms, mr, loc, outs, outr):
    g = lax.axis_index("grid")
    b = lax.axis_index("blk")
    y, z = g // NZ, lax.rem(g, NZ)
    x, c = b // 2, lax.rem(b, 2)

    def side(yv):
        return lax.rem((yv + 1) // 2, 2)

    def partner(yv):
        return yv + 1 - 2 * lax.rem(yv, 2)

    def order(yv, zv):
        return side(yv) * 8 + (yv // 2) * 4 + zv

    s = side(y)
    t = 1 - s
    gp = partner(y) * NZ + z
    gcls = (gp, g)
    pair = (gp, b)
    across = ((3 - y) * NZ + z, b)
    sib = x * 2 + (1 - c)

    def bid(dx):
        return wrap(x + dx) * 2 + c

    def sb(dx):
        return wrap(x + dx) * 2 + (1 - c)

    def zdev(d):
        return (y * NZ + wrap(z + d), b)

    slots = (slots0, slots1)
    bp, bx, outp = (bp0, bp1), (bx0, bx1), (outp0, outp1)
    accs = ((accp0, accp1), (acco0, acco1))

    code = rows_ref[...] * NK + cols_ref[...]
    cap_at = lax.broadcasted_iota(jnp.int32, (CAP, 16), 0)
    code = jnp.where(cap_at < cnt_ref[...], code, -1)
    mine[...] = jnp.full((1, 128), -1, jnp.int32)
    for cap in range(CAP):
        mine[:, cap * 16:cap * 16 + 16] = code[cap:cap + 1]
    mine[:, 32:32 + RB] = owned_ref[...]
    for k in (0, 1):
        slots[k][NONE] = jnp.zeros((BS, BS), BF16)

    bar = pltpu.get_barrier_semaphore()

    @pl.loop(1, 16)
    def _(j):
        q = lax.rem(g + j, 16)
        pl.semaphore_signal(bar, 1, device_id=(q, b), device_id_type=MESH)

    for other in (bid(1), bid(-1), sib):
        pl.semaphore_signal(bar, 1, device_id=(g, other), device_id_type=MESH)
    pl.semaphore_wait(bar, 18)

    def start(src, dst, ssem, rsem, dev):
        pltpu.make_async_remote_copy(
            src_ref=src, dst_ref=dst, send_sem=ssem, recv_sem=rsem,
            device_id=dev, device_id_type=MESH).start()

    def arrive(ref, sem):
        pltpu.make_async_copy(ref, ref, sem).wait()

    def k0(yv, zv):
        return (yv // 2) * 8 + zv * 2

    def breg(n, yv, zv, part):
        lo, cnt = {
            "w": (0, R1), "wa": (0, R1 // 2), "wb": (R1 // 2, R1 // 2),
            "z": (R1, ROWS - R1), "za": (R1, (ROWS - R1) // 2),
            "zb": (R1 + (ROWS - R1) // 2, (ROWS - R1) // 2),
        }[part]
        return bp[n].at[pl.ds(k0(yv, zv), 2), pl.ds(lo, cnt)]

    def chunk(k, b0, s0, lo=0, n=CH):
        return slots[k].at[pl.ds(b0 * 32 + s0 * CH + lo, n)]

    def bsend(label, ref, dev):
        i = B_LABELS.at[label]
        start(ref, ref, bs.at[i], br.at[i], dev)

    def bgot(label, ref):
        arrive(ref, br.at[B_LABELS.at[label]])

    def xsend(label, ref, d):
        i = X_LABELS.at[label]
        start(ref, ref, xs.at[i], xr.at[i], (g, bid(d)))

    def xgot(label, ref):
        arrive(ref, xr.at[X_LABELS.at[label]])

    def psend(label, k, *where):
        i = P_LABELS.at[label]
        start(chunk(k, *where), chunk(1 - k, *where), ps.at[i], pr.at[i], pair)

    def pgot(label, ref):
        arrive(ref, pr.at[P_LABELS.at[label]])

    def csend(label, ref):
        i = C_LABELS.at[label]
        start(ref, ref, cs.at[i], cr.at[i], (g, sib))

    def cgot(label, ref):
        arrive(ref, cr.at[C_LABELS.at[label]])

    here = order(y, z) * CAP

    def a_dst(k):
        return slots[k].at[pl.ds(b * 32 + here, CAP)]

    def a_send(k):
        for j, (far, dz) in enumerate(PIECES):
            yv, zv = (3 - y if far else y), wrap(z + dz)
            owner = (partner(yv) if k == 0 else yv) * NZ + zv
            src = a_ref.at[pl.ds(owner * CAP, CAP)]
            rsem = a1r.at[j] if k == 0 else a1r.at[8]
            if j == 0:
                pltpu.make_async_copy(src, a_dst(k), loc.at[6 + k]).start()
            else:
                start(src, a_dst(k), a1s.at[k], rsem, (yv * NZ + zv, b))

    def piece(j, b0):
        far, dz = PIECES[j]
        at = order(3 - y if far else y, wrap(z - dz)) * CAP
        return slots0.at[pl.ds(b0 * 32 + at, CAP)]

    def x_pieces(js):
        for j in js:
            arrive(piece(j, b), loc.at[6] if j == 0 else a1r.at[j])
            for d in (1, -1):
                xsend(("piece", j, d), piece(j, b), d)

    kown = k0(y, z) + lax.rem(y, 2)

    def b_cols(side_at, n):
        return pl.ds(pl.multiple_of(side_at * 512 + LEFT[n], 128), WIDTH[n])

    a_send(0)
    own_b, cross_b = [], []
    for n in (0, 1):
        cp = pltpu.make_async_copy(b_ref.at[:, b_cols(t, n)], bx[n], loc.at[n])
        cp.start()
        cross_b.append(cp)
    for n in (0, 1):
        cp = pltpu.make_async_copy(b_ref.at[:, b_cols(s, n)], bp[n].at[kown], loc.at[2 + n])
        cp.start()
        own_b.append(cp)
    for n in (0, 1):
        cross_b[n].wait()
        i = B_LABELS.at[(n, "cross")]
        start(bx[n], bp[n].at[kown], bs.at[i], br.at[i], pair)

    @pl.loop(1, 16)
    def _(j):
        q = lax.rem(g + j, 16)
        start(mine, mland.at[b * 16 + g], ms, mr, (q, b))

    pltpu.make_async_copy(mine, mland.at[b * 16 + g], loc.at[8]).start()

    kpair = k0(y, z) + 1 - lax.rem(y, 2)

    def b_start(n):
        own_b[n].wait()
        bgot((n, "cross"), bp[n].at[kpair])
        bsend((n, "w1"), breg(n, y, z, "w"), across)
        for d in (1, -1):
            bsend((n, "z1own", d), breg(n, y, z, "w"), zdev(d))
        for d in (1, -1):
            bsend((n, "y1own", d), breg(n, y, z, "z"), zdev(d))
        bsend((n, "w2own"), breg(n, y, z, "z"), across)

    HALF = {1: "a", -1: "b"}

    def b_step1(n):
        bgot((n, "w1"), breg(n, 3 - y, z, "w"))
        for d in (1, -1):
            bsend((n, "z1far", d), breg(n, 3 - y, z, "w"), zdev(d))
        for d in (1, -1):
            bgot((n, "z1own", d), breg(n, y, wrap(z - d), "w"))
            bsend((n, "z2own", d), breg(n, y, wrap(z - d), "w" + HALF[d]), zdev(d))

    def b_step2(n):
        for d in (1, -1):
            bgot((n, "y1own", d), breg(n, y, wrap(z - d), "z"))
            bsend((n, "w2", d), breg(n, y, wrap(z - d), "z"), across)
            bsend((n, "y2own", d), breg(n, y, wrap(z - d), "z" + HALF[d]), zdev(d))

    def b_step3(n):
        for d in (1, -1):
            bgot((n, "z1far", d), breg(n, 3 - y, wrap(z - d), "w"))
            bsend((n, "z2far", d), breg(n, 3 - y, wrap(z - d), "w" + HALF[d]), zdev(d))
        for d in (1, -1):
            bgot((n, "y2own", d), breg(n, y, wrap(z + 2), "z" + HALF[d]))
            bsend((n, "w2" + HALF[d]), breg(n, y, wrap(z + 2), "z" + HALF[d]), across)

    def b_got_q(n, q):
        if q == 0:
            bgot((n, "w2own"), breg(n, 3 - y, z, "z"))
        elif q < 3:
            d = -1 if q == 1 else 1
            bgot((n, "w2", d), breg(n, 3 - y, wrap(z - d), "z"))
        else:
            for d in (1, -1):
                bgot((n, "z2own", d), breg(n, y, wrap(z + 2), "w" + HALF[d]))
                bgot((n, "z2far", d), breg(n, 3 - y, wrap(z + 2), "w" + HALF[d]))
                bgot((n, "w2" + HALF[d]), breg(n, 3 - y, wrap(z + 2), "z" + HALF[d]))

    def item(k, i, b0, part="all"):
        s0, n = (s, CH) if i == "O" else (t, SF if k == 1 else CH)
        h = n // 2
        lo, cnt = {"all": (0, n), "a": (0, h), "b": (h, n - h)}[part]
        return chunk(k, b0, s0, lo, cnt)

    def x_full(k, i):
        for d in (1, -1):
            xsend((k, i, "full", d), item(k, i, b), d)
        csend((k, i, "own"), item(k, i, b))

    def x_part(part):
        for d in (1, -1):
            xsend((1, "O", "full" + part, d), item(1, "O", b, part), d)

    def x_fwd(k, i):
        for d in (1, -1):
            if (k, i) == (0, "O"):
                for j in range(8):
                    xgot(("piece", j, d), piece(j, bid(-d)))
            elif (k, i) == (1, "O"):
                for part in "ab":
                    xgot((k, i, "full" + part, d), item(k, i, bid(-d), part))
            else:
                xgot((k, i, "full", d), item(k, i, bid(-d)))
            xsend((k, i, "fwd", d), item(k, i, bid(-d), HALF[d]), d)
            csend((k, i, "xp" if d == 1 else "xm"), item(k, i, bid(-d)))

    def x_last(k, i):
        for d in (1, -1):
            xgot((k, i, "fwd", d), item(k, i, bid(2), HALF[d]))
            csend((k, i, "fp" if d == 1 else "fm"), item(k, i, bid(2), HALF[d]))

    def c_end(k, i):
        cgot((k, i, "own"), item(k, i, sb(0)))
        cgot((k, i, "xp"), item(k, i, sb(-1)))
        cgot((k, i, "xm"), item(k, i, sb(1)))
        cgot((k, i, "fp"), item(k, i, sb(2), "a"))
        cgot((k, i, "fm"), item(k, i, sb(2), "b"))

    def p_rest():
        for d in (0, 1, -1, 2):
            psend(("pf", d), 0, bid(d), s, SF, CH - SF)

    def p_rest_got():
        for d in (0, 1, -1, 2):
            ref = chunk(1, bid(d), t, SF, CH - SF)
            pgot(("pf", d), ref)
            csend(("pf", d), ref)

    def c_rest_end():
        for d in (0, 1, -1, 2):
            cgot(("pf", d), chunk(1, sb(d), t, SF, CH - SF))

    def mrow(bb):
        return mland.at[pl.ds(bb * 16, 16)]

    def meta_start():
        pltpu.make_async_copy(mland, msm, loc.at[4]).start()

    def find_all():
        pltpu.make_async_copy(mland, msm, loc.at[4]).wait()
        sub_at = lax.broadcasted_iota(jnp.int32, (RB, 128), 0)
        lane_at = lax.broadcasted_iota(jnp.int32, (RB, 128), 1)
        wants = []
        for k in (0, 1):
            want = lane_at
            for i in range(RB):
                want = jnp.where(sub_at == i, msm[b * 16 + gcls[k], 0, 32 + i] * NK + lane_at, want)
            wants.append(jnp.where(lane_at < NK, want, -2))

        def find(b0, where):
            out = []
            for k in (0, 1):
                w = where[k]
                base = b0 * 32
                for g0 in range(16):
                    yv, zv = g0 // NZ, g0 % NZ
                    at = (((yv + 1) // 2) % 2 * 8 + (yv // 2) * 4 + zv) * CAP
                    for cap in range(CAP):
                        w = jnp.where(wants[k] == msm[b0 * 16 + g0, 0, cap * 16 + gcls[k]], base + at + cap, w)
                out.append(w)
            return tuple(out)

        none = jnp.full((RB, 128), NONE, jnp.int32)
        found = lax.fori_loop(0, 8, find, (none, none))
        for k in (0, 1):
            idxv[k] = found[k]
        idx_copy = pltpu.make_async_copy(idxv, idxs, loc.at[5])
        idx_copy.start()
        idx_copy.wait()

    DZ = (0, 1, -1, 2)

    def dot(k, n, q, rows=(0, RB)):
        zv = wrap(z + DZ[q])
        kbs = [k0(y, zv), k0(y, zv) + 1, k0(3 - y, zv), k0(3 - y, zv) + 1]
        lhs = []
        for i in range(*rows):
            blocks = []
            for kb in kbs:
                gb = ((kb // 8) * 2 + lax.rem(kb, 2)) * NZ + lax.rem(kb, 8) // 2
                blocks += [slots[k][idxs[k, i, gb * 4 + kk]] for kk in range(4)]
            lhs.append(jnp.concatenate(blocks, axis=1))
        rhs = jnp.concatenate(
            [bp[n][pl.ds(kb, 2)].reshape(2 * ROWS, WIDTH[n]) for kb in (kbs[0], kbs[2])], axis=0)
        return jnp.dot(jnp.concatenate(lhs, axis=0), rhs, preferred_element_type=F32)

    def add(k, n, q, rows=(0, RB)):
        lo, hi = rows[0] * BS, rows[1] * BS
        part = dot(k, n, q, rows)
        acc = accs[k][n]
        if q == 0:
            acc[lo:hi] = part
        elif q < 3:
            acc[lo:hi] += part
        elif k == 0:
            outp[n][lo:hi] = (acc[lo:hi] + part).astype(BF16)
        else:
            o_ref[lo:hi, b_cols(s, n)] = (acc[lo:hi] + part).astype(BF16)

    SWAPS = ((0, 0, 8), (1, 0, 4), (1, 4, 8))

    def swap(j):
        n, lo, hi = SWAPS[j]
        add(0, n, 3, (lo, hi))
        rows = pl.ds(lo * BS, (hi - lo) * BS)
        start(outp[n].at[rows], o_ref.at[rows, b_cols(s, n)], outs.at[j], outr.at[j], pair)

    x_pieces((0, 1, 2, 3))
    a_send(1)
    x_pieces((4, 5, 6, 7))
    csend((0, "O", "own"), item(0, "O", b))
    b_start(0)
    arrive(a_dst(1), loc.at[7])
    arrive(slots1.at[pl.ds(0, 14)], a1r.at[8])
    for k in (1, 0):
        psend(("pa", k), k, b, s, 0, SF if k == 0 else CH)
    csend((1, "O", "own"), item(1, "O", b))
    x_fwd(0, "O")
    x_part("a")
    arrive(mland.at[b * 16 + g], loc.at[8])
    arrive(mland.at[pl.ds(0, 15)], mr)
    for d in (1, -1):
        xsend(("meta", d), mrow(b), d)
    csend("m0", mrow(b))
    b_step1(0)
    x_last(0, "O")
    p_rest()
    pgot(("pa", 1), item(0, "Q", b))
    x_full(0, "Q")
    b_step2(0)
    b_start(1)
    for d in (1, -1):
        xgot(("meta", d), mrow(bid(-d)))
        csend("mp" if d == 1 else "mm", mrow(bid(-d)))
    xsend(("metafwd", 1), mrow(bid(-1)), 1)
    b_step3(0)
    x_fwd(0, "Q")
    x_part("b")
    xgot(("metafwd", 1), mrow(bid(2)))
    csend("mf", mrow(bid(2)))
    cgot("m0", mrow(sb(0)))
    cgot("mp", mrow(sb(-1)))
    cgot("mm", mrow(sb(1)))
    cgot("mf", mrow(sb(2)))
    meta_start()
    pgot(("pa", 0), item(1, "Q", b))
    x_full(1, "Q")
    x_last(0, "Q")
    b_step1(1)
    find_all()
    for i in "OQ":
        c_end(0, i)
    b_step2(1)
    b_got_q(0, 0)
    add(0, 0, 0)
    x_fwd(1, "O")
    b_got_q(0, 1)
    add(0, 0, 1)
    b_got_q(0, 2)
    add(0, 0, 2)
    x_fwd(1, "Q")
    b_got_q(0, 3)
    swap(0)
    p_rest_got()
    b_step3(1)
    x_last(1, "O")
    b_got_q(1, 0)
    add(0, 1, 0)
    b_got_q(1, 1)
    add(0, 1, 1)
    b_got_q(1, 2)
    add(0, 1, 2)
    x_last(1, "Q")
    b_got_q(1, 3)
    swap(1)
    swap(2)
    for i in "OQ":
        c_end(1, i)
    c_rest_end()
    add(1, 0, 0)
    add(1, 0, 1)
    add(1, 0, 2)
    add(1, 0, 3)
    add(1, 1, 0)
    add(1, 1, 1)
    add(1, 1, 2)
    add(1, 1, 3)

    for j, (n, lo, hi) in enumerate(SWAPS):
        arrive(o_ref.at[pl.ds(lo * BS, (hi - lo) * BS), b_cols(t, n)], outr.at[j])

    for k in (0, 1):
        arrive(slots[k].at[pl.ds(0, 14)], a1s.at[k])
    arrive(mland.at[pl.ds(0, 15)], ms)
    sizes = {"cross": "x", "w1": "w", "z1own": "w", "z1far": "w", "z2own": "wa", "z2far": "wa",
             "y1own": "z", "y2own": "za", "w2own": "z", "w2": "z", "w2a": "za", "w2b": "zb"}
    for name, i in B_LABELS.at.items():
        part = sizes[name[1]]
        arrive(bx[name[0]] if part == "x" else breg(name[0], 0, 0, part), bs.at[i])
    for name, i in X_LABELS.at.items():
        if name[0] in ("meta", "metafwd"):
            arrive(mrow(b), xs.at[i])
        elif name[0] == "piece":
            arrive(piece(0, b), xs.at[i])
        else:
            k, it, kind, d = name
            arrive(item(k, it, b, {"full": "all", "fwd": HALF[d]}.get(kind, kind[-1])), xs.at[i])
    for name, i in P_LABELS.at.items():
        arrive(chunk(0, 0, 0, 0, {("pa", 0): SF, ("pa", 1): CH}.get(name, CH - SF)), ps.at[i])
    for name, i in C_LABELS.at.items():
        if isinstance(name, str):
            arrive(mrow(b), cs.at[i])
        elif name[0] == "pf":
            arrive(chunk(0, 0, 0, 0, CH - SF), cs.at[i])
        else:
            part = {"own": "all", "xp": "all", "xm": "all", "fp": "a", "fm": "b"}[name[2]]
            arrive(item(name[0], name[1], b, part), cs.at[i])
    for j, (n, lo, hi) in enumerate(SWAPS):
        arrive(outp[n].at[pl.ds(lo * BS, (hi - lo) * BS)], outs.at[j])


def body(a_slots, a_rows, a_cols, a_count, owned_rows, b_matrix):
    DMA = pltpu.SemaphoreType.DMA
    any_space = pl.BlockSpec(memory_space=pl.ANY)
    vmem = pl.BlockSpec(memory_space=pltpu.VMEM)
    return pl.pallas_call(
        kernel,
        out_shape=pltpu.VMEM((RB * BS, b_matrix.shape[1]), BF16),
        in_specs=[any_space, vmem, vmem, vmem, vmem, any_space],
        out_specs=vmem,
        scratch_shapes=[
            *[pltpu.VMEM((16, ROWS, w), BF16) for w in WIDTH],
            *[pltpu.VMEM((ROWS, w), BF16) for w in WIDTH],
            pltpu.VMEM((NONE + 1, BS, BS), BF16),
            pltpu.VMEM((NONE + 1, BS, BS), BF16),
            *[pltpu.VMEM((RB * BS, w), F32) for w in WIDTH * 2],
            *[pltpu.VMEM((RB * BS, w), BF16) for w in WIDTH],
            pltpu.VMEM((1, 128), jnp.int32),
            pltpu.VMEM((128, 1, 128), jnp.int32),
            pltpu.SMEM((128, 1, 128), jnp.int32),
            pltpu.VMEM((2, RB, 128), jnp.int32),
            pltpu.SMEM((2, RB, 128), jnp.int32),
            DMA((len(B_LABELS),)), DMA((len(B_LABELS),)),
            DMA((len(X_LABELS),)), DMA((len(X_LABELS),)),
            DMA((len(P_LABELS),)), DMA((len(P_LABELS),)),
            DMA((len(C_LABELS),)), DMA((len(C_LABELS),)),
            DMA((2,)), DMA((9,)), DMA, DMA, DMA((9,)), DMA((3,)), DMA((3,)),
        ],
        compiler_params=pltpu.CompilerParams(
            collective_id=0, has_side_effects=True, vmem_limit_bytes=60 << 20),
    )(
        a_slots.reshape(16 * CAP, BS, BS),
        a_rows.reshape(16, CAP).T,
        a_cols.reshape(16, CAP).T,
        a_count.reshape(1, 16),
        owned_rows,
        b_matrix,
    )


def solution(mesh):
    in_specs = (
        P("grid", "blk", None, None, None, None),
        P("grid", "blk", None, None),
        P("grid", "blk", None, None),
        P("grid", "blk", None),
        P("grid", None),
        P("grid", "blk"),
    )
    return jax.shard_map(body, mesh=mesh, in_specs=in_specs, out_specs=P("grid", "blk"), check_vma=False)
```

```python
import jax
import jax.numpy as jnp
from jax import lax
from jax.experimental import pallas as pl
from jax.experimental.pallas import tpu as pltpu
from jax.sharding import PartitionSpec as P

CAP = 2
RB = 8
BS = 128
NZ = 4
NK = 64
WIDTH = (256, 256)
LEFT = (0, 256)
CH = 16
SF = 9
R1 = 288
ROWS = 512
NONE = 256
PIECES = ((0, 0), (0, 1), (0, 3), (1, 0), (0, 2), (1, 1), (1, 3), (1, 2))
MESH = pl.DeviceIdType.MESH
F32 = jnp.float32
BF16 = jnp.bfloat16


def wrap(v):
    return lax.rem(v + 4, 4)


class Labels:
    def __init__(self, names):
        self.at = {n: i for i, n in enumerate(names)}

    def __len__(self):
        return len(self.at)


B_LABELS = Labels(
    [(n, k) for n in (0, 1) for k in ("cross", "w1", "w2own", "w2a", "w2b")]
    + [(n, k, s) for n in (0, 1) for s in (1, -1)
       for k in ("z1own", "z1far", "z2own", "z2far", "y1own", "y2own", "w2")]
)
X_LABELS = Labels(
    [(k, i, t, s) for k in (0, 1) for i in "OQ" for t in ("full", "fwd") for s in (1, -1)
     if (k, i, t) not in ((0, "O", "full"), (1, "O", "full"))]
    + [(1, "O", t, s) for t in ("fulla", "fullb") for s in (1, -1)]
    + [("piece", j, s) for j in range(8) for s in (1, -1)]
    + [("meta", 1), ("meta", -1), ("metafwd", 1)]
)
P_LABELS = Labels([("pa", k) for k in (0, 1)] + [("pf", d) for d in (0, 1, -1, 2)])
C_LABELS = Labels(
    [(k, i, t) for k in (0, 1) for i in "OQ" for t in ("own", "xp", "xm", "fp", "fm")]
    + [("pf", d) for d in (0, 1, -1, 2)]
    + ["m0", "mp", "mm", "mf"]
)


def kernel(a_ref, rows_ref, cols_ref, cnt_ref, owned_ref, b_ref, o_ref,
           bp0, bp1, bx0, bx1, slots0, slots1, accp0, accp1, acco0, acco1, outp0, outp1, mine, mland, msm, idxv, idxs,
           bs, br, xs, xr, ps, pr, cs, cr, a1s, a1r, ms, mr, loc, outs, outr):
    g = lax.axis_index("grid")
    b = lax.axis_index("blk")
    y, z = g // NZ, lax.rem(g, NZ)
    x, c = b // 2, lax.rem(b, 2)

    def side(yv):
        return lax.rem((yv + 1) // 2, 2)

    def partner(yv):
        return yv + 1 - 2 * lax.rem(yv, 2)

    def order(yv, zv):
        return side(yv) * 8 + (yv // 2) * 4 + zv

    s = side(y)
    t = 1 - s
    gp = partner(y) * NZ + z
    gcls = (gp, g)
    pair = (gp, b)
    across = ((3 - y) * NZ + z, b)
    sib = x * 2 + (1 - c)

    def bid(dx):
        return wrap(x + dx) * 2 + c

    def sb(dx):
        return wrap(x + dx) * 2 + (1 - c)

    def zdev(d):
        return (y * NZ + wrap(z + d), b)

    slots = (slots0, slots1)
    bp, bx, outp = (bp0, bp1), (bx0, bx1), (outp0, outp1)
    accs = ((accp0, accp1), (acco0, acco1))

    code = rows_ref[...] * NK + cols_ref[...]
    cap_at = lax.broadcasted_iota(jnp.int32, (CAP, 16), 0)
    code = jnp.where(cap_at < cnt_ref[...], code, -1)
    mine[...] = jnp.full((1, 128), -1, jnp.int32)
    for cap in range(CAP):
        mine[:, cap * 16:cap * 16 + 16] = code[cap:cap + 1]
    mine[:, 32:32 + RB] = owned_ref[...]
    for k in (0, 1):
        slots[k][NONE] = jnp.zeros((BS, BS), BF16)

    bar = pltpu.get_barrier_semaphore()

    @pl.loop(1, 16)
    def _(j):
        q = lax.rem(g + j, 16)
        pl.semaphore_signal(bar, 1, device_id=(q, b), device_id_type=MESH)

    for other in (bid(1), bid(-1), sib):
        pl.semaphore_signal(bar, 1, device_id=(g, other), device_id_type=MESH)
    pl.semaphore_wait(bar, 18)

    def start(src, dst, ssem, rsem, dev):
        pltpu.make_async_remote_copy(
            src_ref=src, dst_ref=dst, send_sem=ssem, recv_sem=rsem,
            device_id=dev, device_id_type=MESH).start()

    def arrive(ref, sem):
        pltpu.make_async_copy(ref, ref, sem).wait()

    def k0(yv, zv):
        return (yv // 2) * 8 + zv * 2

    def breg(n, yv, zv, part):
        lo, cnt = {
            "w": (0, R1), "wa": (0, R1 // 2), "wb": (R1 // 2, R1 // 2),
            "z": (R1, ROWS - R1), "za": (R1, (ROWS - R1) // 2),
            "zb": (R1 + (ROWS - R1) // 2, (ROWS - R1) // 2),
        }[part]
        return bp[n].at[pl.ds(k0(yv, zv), 2), pl.ds(lo, cnt)]

    def chunk(k, b0, s0, lo=0, n=CH):
        return slots[k].at[pl.ds(b0 * 32 + s0 * CH + lo, n)]

    def bsend(label, ref, dev):
        i = B_LABELS.at[label]
        start(ref, ref, bs.at[i], br.at[i], dev)

    def bgot(label, ref):
        arrive(ref, br.at[B_LABELS.at[label]])

    def xsend(label, ref, d):
        i = X_LABELS.at[label]
        start(ref, ref, xs.at[i], xr.at[i], (g, bid(d)))

    def xgot(label, ref):
        arrive(ref, xr.at[X_LABELS.at[label]])

    def psend(label, k, *where):
        i = P_LABELS.at[label]
        start(chunk(k, *where), chunk(1 - k, *where), ps.at[i], pr.at[i], pair)

    def pgot(label, ref):
        arrive(ref, pr.at[P_LABELS.at[label]])

    def csend(label, ref):
        i = C_LABELS.at[label]
        start(ref, ref, cs.at[i], cr.at[i], (g, sib))

    def cgot(label, ref):
        arrive(ref, cr.at[C_LABELS.at[label]])

    here = order(y, z) * CAP

    def a_dst(k):
        return slots[k].at[pl.ds(b * 32 + here, CAP)]

    def a_send(k):
        for j, (far, dz) in enumerate(PIECES):
            yv, zv = (3 - y if far else y), wrap(z + dz)
            owner = (partner(yv) if k == 0 else yv) * NZ + zv
            src = a_ref.at[pl.ds(owner * CAP, CAP)]
            rsem = a1r.at[j] if k == 0 else a1r.at[8]
            if j == 0:
                pltpu.make_async_copy(src, a_dst(k), loc.at[6 + k]).start()
            else:
                start(src, a_dst(k), a1s.at[k], rsem, (yv * NZ + zv, b))

    def piece(j, b0):
        far, dz = PIECES[j]
        at = order(3 - y if far else y, wrap(z - dz)) * CAP
        return slots0.at[pl.ds(b0 * 32 + at, CAP)]

    def x_pieces(js):
        for j in js:
            arrive(piece(j, b), loc.at[6] if j == 0 else a1r.at[j])
            for d in (1, -1):
                xsend(("piece", j, d), piece(j, b), d)

    kown = k0(y, z) + lax.rem(y, 2)

    def b_cols(side_at, n):
        return pl.ds(pl.multiple_of(side_at * 512 + LEFT[n], 128), WIDTH[n])

    own_b, cross_b = [], []
    for n in (0, 1):
        cp = pltpu.make_async_copy(b_ref.at[:, b_cols(t, n)], bx[n], loc.at[n])
        cp.start()
        cross_b.append(cp)
    for n in (0, 1):
        cp = pltpu.make_async_copy(b_ref.at[:, b_cols(s, n)], bp[n].at[kown], loc.at[2 + n])
        cp.start()
        own_b.append(cp)
    a_send(0)
    for n in (0, 1):
        cross_b[n].wait()
        i = B_LABELS.at[(n, "cross")]
        start(bx[n], bp[n].at[kown], bs.at[i], br.at[i], pair)
    a_send(1)

    @pl.loop(1, 16)
    def _(j):
        q = lax.rem(g + j, 16)
        start(mine, mland.at[b * 16 + g], ms, mr, (q, b))

    pltpu.make_async_copy(mine, mland.at[b * 16 + g], loc.at[8]).start()

    kpair = k0(y, z) + 1 - lax.rem(y, 2)

    def b_start(n):
        own_b[n].wait()
        bgot((n, "cross"), bp[n].at[kpair])
        bsend((n, "w1"), breg(n, y, z, "w"), across)
        for d in (1, -1):
            bsend((n, "z1own", d), breg(n, y, z, "w"), zdev(d))
        for d in (1, -1):
            bsend((n, "y1own", d), breg(n, y, z, "z"), zdev(d))
        bsend((n, "w2own"), breg(n, y, z, "z"), across)

    HALF = {1: "a", -1: "b"}

    def b_step1(n):
        bgot((n, "w1"), breg(n, 3 - y, z, "w"))
        for d in (1, -1):
            bsend((n, "z1far", d), breg(n, 3 - y, z, "w"), zdev(d))
        for d in (1, -1):
            bgot((n, "z1own", d), breg(n, y, wrap(z - d), "w"))
            bsend((n, "z2own", d), breg(n, y, wrap(z - d), "w" + HALF[d]), zdev(d))

    def b_step2(n):
        for d in (1, -1):
            bgot((n, "y1own", d), breg(n, y, wrap(z - d), "z"))
            bsend((n, "w2", d), breg(n, y, wrap(z - d), "z"), across)
            bsend((n, "y2own", d), breg(n, y, wrap(z - d), "z" + HALF[d]), zdev(d))

    def b_step3(n):
        for d in (1, -1):
            bgot((n, "z1far", d), breg(n, 3 - y, wrap(z - d), "w"))
            bsend((n, "z2far", d), breg(n, 3 - y, wrap(z - d), "w" + HALF[d]), zdev(d))
        for d in (1, -1):
            bgot((n, "y2own", d), breg(n, y, wrap(z + 2), "z" + HALF[d]))
            bsend((n, "w2" + HALF[d]), breg(n, y, wrap(z + 2), "z" + HALF[d]), across)

    def b_got_q(n, q):
        if q == 0:
            bgot((n, "w2own"), breg(n, 3 - y, z, "z"))
        elif q < 3:
            d = -1 if q == 1 else 1
            bgot((n, "w2", d), breg(n, 3 - y, wrap(z - d), "z"))
        else:
            for d in (1, -1):
                bgot((n, "z2own", d), breg(n, y, wrap(z + 2), "w" + HALF[d]))
                bgot((n, "z2far", d), breg(n, 3 - y, wrap(z + 2), "w" + HALF[d]))
                bgot((n, "w2" + HALF[d]), breg(n, 3 - y, wrap(z + 2), "z" + HALF[d]))

    def item(k, i, b0, part="all"):
        s0, n = (s, CH) if i == "O" else (t, SF if k == 1 else CH)
        h = n // 2
        lo, cnt = {"all": (0, n), "a": (0, h), "b": (h, n - h)}[part]
        return chunk(k, b0, s0, lo, cnt)

    def x_full(k, i):
        for d in (1, -1):
            xsend((k, i, "full", d), item(k, i, b), d)
        csend((k, i, "own"), item(k, i, b))

    def x_part(part):
        for d in (1, -1):
            xsend((1, "O", "full" + part, d), item(1, "O", b, part), d)

    def x_fwd(k, i):
        for d in (1, -1):
            if (k, i) == (0, "O"):
                for j in range(8):
                    xgot(("piece", j, d), piece(j, bid(-d)))
            elif (k, i) == (1, "O"):
                for part in "ab":
                    xgot((k, i, "full" + part, d), item(k, i, bid(-d), part))
            else:
                xgot((k, i, "full", d), item(k, i, bid(-d)))
            xsend((k, i, "fwd", d), item(k, i, bid(-d), HALF[d]), d)
            csend((k, i, "xp" if d == 1 else "xm"), item(k, i, bid(-d)))

    def x_last(k, i):
        for d in (1, -1):
            xgot((k, i, "fwd", d), item(k, i, bid(2), HALF[d]))
            csend((k, i, "fp" if d == 1 else "fm"), item(k, i, bid(2), HALF[d]))

    def c_end(k, i):
        cgot((k, i, "own"), item(k, i, sb(0)))
        cgot((k, i, "xp"), item(k, i, sb(-1)))
        cgot((k, i, "xm"), item(k, i, sb(1)))
        cgot((k, i, "fp"), item(k, i, sb(2), "a"))
        cgot((k, i, "fm"), item(k, i, sb(2), "b"))

    def p_rest():
        for d in (0, 1, -1, 2):
            psend(("pf", d), 0, bid(d), s, SF, CH - SF)

    def p_rest_got():
        for d in (0, 1, -1, 2):
            ref = chunk(1, bid(d), t, SF, CH - SF)
            pgot(("pf", d), ref)
            csend(("pf", d), ref)

    def c_rest_end():
        for d in (0, 1, -1, 2):
            cgot(("pf", d), chunk(1, sb(d), t, SF, CH - SF))

    def mrow(bb):
        return mland.at[pl.ds(bb * 16, 16)]

    def meta_start():
        pltpu.make_async_copy(mland, msm, loc.at[4]).start()

    def find_all():
        pltpu.make_async_copy(mland, msm, loc.at[4]).wait()
        sub_at = lax.broadcasted_iota(jnp.int32, (RB, 128), 0)
        lane_at = lax.broadcasted_iota(jnp.int32, (RB, 128), 1)
        wants = []
        for k in (0, 1):
            want = lane_at
            for i in range(RB):
                want = jnp.where(sub_at == i, msm[b * 16 + gcls[k], 0, 32 + i] * NK + lane_at, want)
            wants.append(jnp.where(lane_at < NK, want, -2))

        def find(b0, where):
            out = []
            for k in (0, 1):
                w = where[k]
                base = b0 * 32
                for g0 in range(16):
                    yv, zv = g0 // NZ, g0 % NZ
                    at = (((yv + 1) // 2) % 2 * 8 + (yv // 2) * 4 + zv) * CAP
                    for cap in range(CAP):
                        w = jnp.where(wants[k] == msm[b0 * 16 + g0, 0, cap * 16 + gcls[k]], base + at + cap, w)
                out.append(w)
            return tuple(out)

        none = jnp.full((RB, 128), NONE, jnp.int32)
        found = lax.fori_loop(0, 8, find, (none, none))
        for k in (0, 1):
            idxv[k] = found[k]
        idx_copy = pltpu.make_async_copy(idxv, idxs, loc.at[5])
        idx_copy.start()
        idx_copy.wait()

    DZ = (0, 1, -1, 2)

    def dot(k, n, q, rows=(0, RB)):
        zv = wrap(z + DZ[q])
        kbs = [k0(y, zv), k0(y, zv) + 1, k0(3 - y, zv), k0(3 - y, zv) + 1]
        lhs = []
        for i in range(*rows):
            blocks = []
            for kb in kbs:
                gb = ((kb // 8) * 2 + lax.rem(kb, 2)) * NZ + lax.rem(kb, 8) // 2
                blocks += [slots[k][idxs[k, i, gb * 4 + kk]] for kk in range(4)]
            lhs.append(jnp.concatenate(blocks, axis=1))
        rhs = jnp.concatenate(
            [bp[n][pl.ds(kb, 2)].reshape(2 * ROWS, WIDTH[n]) for kb in (kbs[0], kbs[2])], axis=0)
        return jnp.dot(jnp.concatenate(lhs, axis=0), rhs, preferred_element_type=F32)

    def add(k, n, q, rows=(0, RB)):
        lo, hi = rows[0] * BS, rows[1] * BS
        part = dot(k, n, q, rows)
        acc = accs[k][n]
        if q == 0:
            acc[lo:hi] = part
        elif q < 3:
            acc[lo:hi] += part
        elif k == 0:
            outp[n][lo:hi] = (acc[lo:hi] + part).astype(BF16)
        else:
            o_ref[lo:hi, b_cols(s, n)] = (acc[lo:hi] + part).astype(BF16)

    SWAPS = ((0, 0, 8), (1, 0, 4), (1, 4, 8))

    def swap(j):
        n, lo, hi = SWAPS[j]
        add(0, n, 3, (lo, hi))
        rows = pl.ds(lo * BS, (hi - lo) * BS)
        start(outp[n].at[rows], o_ref.at[rows, b_cols(s, n)], outs.at[j], outr.at[j], pair)

    x_pieces((0, 1, 2, 3))
    x_pieces((4, 5, 6, 7))
    csend((0, "O", "own"), item(0, "O", b))
    b_start(0)
    arrive(a_dst(1), loc.at[7])
    arrive(slots1.at[pl.ds(0, 14)], a1r.at[8])
    for k in (1, 0):
        psend(("pa", k), k, b, s, 0, SF if k == 0 else CH)
    csend((1, "O", "own"), item(1, "O", b))
    x_fwd(0, "O")
    x_part("a")
    arrive(mland.at[b * 16 + g], loc.at[8])
    arrive(mland.at[pl.ds(0, 15)], mr)
    for d in (1, -1):
        xsend(("meta", d), mrow(b), d)
    csend("m0", mrow(b))
    b_step1(0)
    x_last(0, "O")
    p_rest()
    pgot(("pa", 1), item(0, "Q", b))
    x_full(0, "Q")
    b_step2(0)
    b_start(1)
    for d in (1, -1):
        xgot(("meta", d), mrow(bid(-d)))
        csend("mp" if d == 1 else "mm", mrow(bid(-d)))
    xsend(("metafwd", 1), mrow(bid(-1)), 1)
    b_step3(0)
    x_fwd(0, "Q")
    x_part("b")
    xgot(("metafwd", 1), mrow(bid(2)))
    csend("mf", mrow(bid(2)))
    cgot("m0", mrow(sb(0)))
    cgot("mp", mrow(sb(-1)))
    cgot("mm", mrow(sb(1)))
    cgot("mf", mrow(sb(2)))
    meta_start()
    pgot(("pa", 0), item(1, "Q", b))
    x_full(1, "Q")
    x_last(0, "Q")
    b_step1(1)
    find_all()
    for i in "OQ":
        c_end(0, i)
    b_step2(1)
    b_got_q(0, 0)
    add(0, 0, 0)
    x_fwd(1, "O")
    b_got_q(0, 1)
    add(0, 0, 1)
    b_got_q(0, 2)
    add(0, 0, 2)
    x_fwd(1, "Q")
    b_got_q(0, 3)
    swap(0)
    p_rest_got()
    b_step3(1)
    x_last(1, "O")
    b_got_q(1, 0)
    add(0, 1, 0)
    b_got_q(1, 1)
    add(0, 1, 1)
    b_got_q(1, 2)
    add(0, 1, 2)
    x_last(1, "Q")
    b_got_q(1, 3)
    swap(1)
    swap(2)
    for i in "OQ":
        c_end(1, i)
    c_rest_end()
    add(1, 0, 0)
    add(1, 0, 1)
    add(1, 0, 2)
    add(1, 0, 3)
    add(1, 1, 0)
    add(1, 1, 1)
    add(1, 1, 2)
    add(1, 1, 3)

    for j, (n, lo, hi) in enumerate(SWAPS):
        arrive(o_ref.at[pl.ds(lo * BS, (hi - lo) * BS), b_cols(t, n)], outr.at[j])

    for k in (0, 1):
        arrive(slots[k].at[pl.ds(0, 14)], a1s.at[k])
    arrive(mland.at[pl.ds(0, 15)], ms)
    sizes = {"cross": "x", "w1": "w", "z1own": "w", "z1far": "w", "z2own": "wa", "z2far": "wa",
             "y1own": "z", "y2own": "za", "w2own": "z", "w2": "z", "w2a": "za", "w2b": "zb"}
    for name, i in B_LABELS.at.items():
        part = sizes[name[1]]
        arrive(bx[name[0]] if part == "x" else breg(name[0], 0, 0, part), bs.at[i])
    for name, i in X_LABELS.at.items():
        if name[0] in ("meta", "metafwd"):
            arrive(mrow(b), xs.at[i])
        elif name[0] == "piece":
            arrive(piece(0, b), xs.at[i])
        else:
            k, it, kind, d = name
            arrive(item(k, it, b, {"full": "all", "fwd": HALF[d]}.get(kind, kind[-1])), xs.at[i])
    for name, i in P_LABELS.at.items():
        arrive(chunk(0, 0, 0, 0, {("pa", 0): SF, ("pa", 1): CH}.get(name, CH - SF)), ps.at[i])
    for name, i in C_LABELS.at.items():
        if isinstance(name, str):
            arrive(mrow(b), cs.at[i])
        elif name[0] == "pf":
            arrive(chunk(0, 0, 0, 0, CH - SF), cs.at[i])
        else:
            part = {"own": "all", "xp": "all", "xm": "all", "fp": "a", "fm": "b"}[name[2]]
            arrive(item(name[0], name[1], b, part), cs.at[i])
    for j, (n, lo, hi) in enumerate(SWAPS):
        arrive(outp[n].at[pl.ds(lo * BS, (hi - lo) * BS)], outs.at[j])


def body(a_slots, a_rows, a_cols, a_count, owned_rows, b_matrix):
    DMA = pltpu.SemaphoreType.DMA
    any_space = pl.BlockSpec(memory_space=pl.ANY)
    vmem = pl.BlockSpec(memory_space=pltpu.VMEM)
    return pl.pallas_call(
        kernel,
        out_shape=pltpu.VMEM((RB * BS, b_matrix.shape[1]), BF16),
        in_specs=[any_space, vmem, vmem, vmem, vmem, any_space],
        out_specs=vmem,
        scratch_shapes=[
            *[pltpu.VMEM((16, ROWS, w), BF16) for w in WIDTH],
            *[pltpu.VMEM((ROWS, w), BF16) for w in WIDTH],
            pltpu.VMEM((NONE + 1, BS, BS), BF16),
            pltpu.VMEM((NONE + 1, BS, BS), BF16),
            *[pltpu.VMEM((RB * BS, w), F32) for w in WIDTH * 2],
            *[pltpu.VMEM((RB * BS, w), BF16) for w in WIDTH],
            pltpu.VMEM((1, 128), jnp.int32),
            pltpu.VMEM((128, 1, 128), jnp.int32),
            pltpu.SMEM((128, 1, 128), jnp.int32),
            pltpu.VMEM((2, RB, 128), jnp.int32),
            pltpu.SMEM((2, RB, 128), jnp.int32),
            DMA((len(B_LABELS),)), DMA((len(B_LABELS),)),
            DMA((len(X_LABELS),)), DMA((len(X_LABELS),)),
            DMA((len(P_LABELS),)), DMA((len(P_LABELS),)),
            DMA((len(C_LABELS),)), DMA((len(C_LABELS),)),
            DMA((2,)), DMA((9,)), DMA, DMA, DMA((9,)), DMA((3,)), DMA((3,)),
        ],
        compiler_params=pltpu.CompilerParams(
            collective_id=0, has_side_effects=True, vmem_limit_bytes=60 << 20),
    )(
        a_slots.reshape(16 * CAP, BS, BS),
        a_rows.reshape(16, CAP).T,
        a_cols.reshape(16, CAP).T,
        a_count.reshape(1, 16),
        owned_rows,
        b_matrix,
    )


def solution(mesh):
    in_specs = (
        P("grid", "blk", None, None, None, None),
        P("grid", "blk", None, None),
        P("grid", "blk", None, None),
        P("grid", "blk", None),
        P("grid", None),
        P("grid", "blk"),
    )
    return jax.shard_map(body, mesh=mesh, in_specs=in_specs, out_specs=P("grid", "blk"), check_vma=False)
```
